512 devices in a mesh: row: 32 (over z, core), col: 16 (over y, x).
Axes of the slice: x: 4, y: 4, z: 16, core: 2. Of those that a mesh axis runs over, the one named last changes fastest.
Arguments:
- trailing: bfloat16 [24576, 12288], P('row', 'col'), may hold values from -6 to 6
- offdiagonal_panel_rows: bfloat16 [2, 24576, 512], P(None, ('row', 'col')), may hold values from -3 to 3
- pivot_diagonal_blocks: bfloat16 [2, 512, 512], replicated, may hold values from -3 to 14, as said below
- coupling: bfloat16 [512, 512], replicated, may hold values from -0.3314563 to 0.3314563, as said below
- pattern: int32 [2, 192], replicated, may hold values 0 or 1
- block_slot_lookup: int32 [192], replicated, may hold values from 0 to 191, each once
- elimination_sequence: int32 [2], replicated, may hold values from 0 to 1, each once
Outputs:
- updated: bfloat16 [24576, 12288], P('row', 'col')
- factor: bfloat16 [2, 24576, 512], P(None, ('row', 'col'))
The draws below stay inside these ranges and needn't reach their ends.
Inputs may be any that keep to these rules, and one draw needn't show every extreme that they name: `pivot_diagonal_blocks`: each diagonal block is symmetric positive definite. `coupling`: pivot_diagonal_blocks[b] - link link^T is positive definite. `elimination_sequence`: a permutation of the two panel indices.
All inputs are finite; a program needn't handle non-finite values.
Results may differ from the reference program's by a relative error of at most 0.0055.
Values may be sent and summed in bfloat16 or wider, within the bound.
No kernel may reach another device: no remote copies, remote signals or barrier semaphores. Data moves between devices by JAX's collectives and lax.ppermute only.
A program may use at most 64 MiB of HBM per device.

```python
import jax
import jax.numpy as jnp

B = 128
SN = 512
NB = 192
NC = 96


def draw_pivot_diagonal_blocks(key, part):
    base_key = jax.random.fold_in(key, 3)
    base = jnp.clip(jax.random.normal(base_key, (2, SN, SN), jnp.float32), -3.0, 3.0)
    gram = jnp.einsum('pik,pjk->pij', base, base) / SN
    matrix = 2.0 * jnp.eye(SN, dtype=jnp.float32)[None] + gram
    return matrix.astype(jnp.bfloat16)


def draw_coupling(key, part):
    entry_key = jax.random.fold_in(key, 5)
    spread = 1.05 * SN ** (-0.5)
    raw = jnp.clip(jax.random.normal(entry_key, (SN, SN), jnp.float32), -3.0, 3.0)
    return (raw * spread).astype(jnp.bfloat16)


def set_ends(array, key, smallest, high):
    longest = array.shape.index(max(array.shape))
    spots = []
    for shift in (0, 1):
        where = [jax.random.randint(jax.random.fold_in(key, axis), (), 0, length) for axis, length in enumerate(array.shape)]
        where[longest] = (where[longest] + shift) % array.shape[longest]
        spots.append(tuple(where))
    return array.at[spots[0]].set(smallest).at[spots[1]].set(high)


def levels(own_key, dims, cuts, low, top_value):
    def one(dim, blocks):
        steps = jax.random.uniform(jax.random.fold_in(jax.random.fold_in(own_key, 6), dim), (blocks,), jnp.float32, low / len(cuts), top_value / len(cuts))
        return jnp.repeat(jnp.exp(steps), dims[dim] // blocks).reshape((-1,) + (1,) * (len(dims) - dim - 1))

    gain = one(*cuts[0])
    for cut in cuts[1:]:
        gain = gain * one(*cut)
    return gain


def centred(rng, shape, width, reach, pieces=(), kind=jnp.bfloat16):
    factor_of = levels(rng, shape, pieces, -0.22, 0.18) if pieces else 1.0
    values = jax.random.normal(rng, shape, jnp.float32) * width * factor_of
    return jnp.minimum(jnp.maximum(values, -reach), reach).astype(kind)


def setup_inputs(seed: int = 0) -> dict:
    seeds = jax.random.split(jax.random.key(seed), 8)
    return {
        "trailing": centred(seeds[0], (NB * B, NC * B), 1.0, 6.0, ((0, 32), (1, 16))),
        "offdiagonal_panel_rows": centred(seeds[1], (2, NB * B, SN), 0.4, 3.0, ((1, 512),)),
        "pivot_diagonal_blocks": draw_pivot_diagonal_blocks(jax.random.fold_in(seeds[7], 71), 0),
        "coupling": draw_coupling(jax.random.fold_in(seeds[7], 71), 0),
        "pattern": set_ends((jax.random.randint(seeds[4], (2, NB), 0, 3) < 2).astype(jnp.int32), jax.random.fold_in(seeds[4], 1), 0, 1),
        "block_slot_lookup": jax.random.permutation(seeds[5], NB).astype(jnp.int32),
        "elimination_sequence": jax.random.permutation(seeds[6], 2).astype(jnp.int32),
    }


def solve_right(rhs, lower_factor):
    return jax.scipy.linalg.solve_triangular(lower_factor, rhs.T, lower=True).T

def reference(trailing, offdiagonal_panel_rows, pivot_diagonal_blocks, coupling, pattern, block_slot_lookup, elimination_sequence):
    total_rows = offdiagonal_panel_rows.shape[1]
    slots = (jnp.arange(total_rows, dtype=jnp.int32) // B).astype(jnp.int32)
    global_block = block_slot_lookup[slots]
    keep_mask = pattern[:, global_block].astype(jnp.float32)
    masked = offdiagonal_panel_rows.astype(jnp.float32) * keep_mask[:, :, None]
    exchanged_panels = elimination_sequence[0] == 1
    sorted_panels = jnp.where(exchanged_panels, masked[::-1], masked)
    diagonals = pivot_diagonal_blocks.astype(jnp.float32)
    diagonals = jnp.where(exchanged_panels, diagonals[::-1], diagonals)
    couple = coupling.astype(jnp.float32)
    kmat = jnp.where(exchanged_panels, couple.T, couple)
    first_factor = jnp.linalg.cholesky(diagonals[0])
    leading_rows = solve_right(sorted_panels[0], first_factor).astype(jnp.bfloat16)
    link = solve_right(kmat, first_factor).astype(jnp.bfloat16)
    shrunk = diagonals[1] - jnp.dot(link.astype(jnp.float32), link.T.astype(jnp.float32), preferred_element_type=jnp.float32)
    second_factor = jnp.linalg.cholesky(shrunk)
    updated_rows = sorted_panels[1] - jnp.dot(leading_rows.astype(jnp.float32), link.T.astype(jnp.float32), preferred_element_type=jnp.float32)
    second_rows = solve_right(updated_rows, second_factor).astype(jnp.bfloat16)
    columns = NC * B
    result = trailing.astype(jnp.float32)
    result = result - jnp.dot(leading_rows.astype(jnp.float32), leading_rows[:columns].T.astype(jnp.float32), preferred_element_type=jnp.float32)
    result = result - jnp.dot(second_rows.astype(jnp.float32), second_rows[:columns].T.astype(jnp.float32), preferred_element_type=jnp.float32)
    stacked = jnp.stack([leading_rows, second_rows])
    factor = jnp.where(exchanged_panels, stacked[::-1], stacked)
    return (result.astype(jnp.bfloat16), factor)
```

```python
import functools

import jax
import jax.numpy as jnp
from jax import lax
from jax.experimental import pallas as pl
from jax.experimental.pallas import tpu as pltpu
from jax.sharding import Mesh, PartitionSpec as P

B = 128
STEP = 16
F32 = jnp.float32
BF16 = jnp.bfloat16


VMEM = pl.BlockSpec(memory_space=pltpu.VMEM)
SMEM = pl.BlockSpec(memory_space=pltpu.SMEM)


def dot(left, right, contract_left, contract_right):
    return lax.dot_general(
        left, right, (((contract_left,), (contract_right,)), ((), ())), preferred_element_type=F32
    )


def split(value):
    high = value.astype(BF16)
    return high, (value - high.astype(F32)).astype(BF16)


def dot_split(left, right, contract_left, contract_right):
    left_high, left_low = split(left)
    right_high, right_low = split(right)
    return (
        dot(left_high, right_high, contract_left, contract_right)
        + dot(left_high, right_low, contract_left, contract_right)
        + dot(left_low, right_high, contract_left, contract_right)
    )


def row_of(value, sublane):
    return jnp.broadcast_to(value[sublane : sublane + 1, :], value.shape)


def eliminate(work, inverse, step):
    start = STEP * step
    tiles = STEP // 8
    tile_rows = [pl.ds(start + 8 * h, 8) for h in range(tiles)]
    rows = [[ref[r, :] for r in tile_rows] for ref in (work, inverse)]
    columns = [
        [jnp.broadcast_to(rows[0][h][:, start + j : start + j + 1], (8, B)) for h in range(tiles)]
        for j in range(STEP)
    ]
    sublane = lax.broadcasted_iota(jnp.int32, (8, B), 0)
    zero = jnp.zeros((8, B), F32)
    scale = [zero] * tiles
    for k in range(STEP):
        tile, s = k // 8, k % 8
        root = lax.rsqrt(row_of(columns[k][tile], s))
        inverse_pivot = root * root
        scale[tile] = jnp.where(sublane == s, root, scale[tile])
        below = [(h, columns[k][h]) for h in range(tile + 1, tiles)]
        if s < 7:
            below.append((tile, jnp.where(sublane > s, columns[k][tile], zero)))
        for j in range(k + 1, STEP):
            pivot_row = row_of(columns[j][tile], s)
            if j == k + 1:
                for h, column in below:
                    columns[j][h] = columns[j][h] - (column * pivot_row) * inverse_pivot
            else:
                pivot_row = pivot_row * inverse_pivot
                for h, column in below:
                    columns[j][h] = columns[j][h] - column * pivot_row
        for side in rows:
            pivot_row = row_of(side[tile], s) * inverse_pivot
            for h, column in below:
                side[h] = side[h] - column * pivot_row
    rows = [jnp.concatenate([side[h] * scale[h] for h in range(tiles)], 0) for side in rows]
    work[pl.ds(start, STEP), :] = rows[0]
    inverse[pl.ds(start, STEP), :] = rows[1]
    if start + STEP == B:
        return
    upper_high, upper_low = split(rows[0])
    side_high, side_low = split(rows[1])
    left = jnp.concatenate([upper_high, upper_high, upper_low], 0)
    rest = slice(start + STEP, B)
    change = dot(left, jnp.concatenate([upper_high, upper_low, upper_high], 0), 0, 0)
    work[rest, :] = work[rest, :] - change[rest, :]
    change = dot(left, jnp.concatenate([side_high, side_low, side_high], 0), 0, 0)
    inverse[rest, :] = inverse[rest, :] - change[rest, :]


def factor(matrix, inverse, block_work, block_inverse):
    size = matrix.shape[0]
    inverse[...] = jnp.zeros(inverse.shape, F32)
    row = lax.broadcasted_iota(jnp.int32, (B, B), 0)
    column = lax.broadcasted_iota(jnp.int32, (B, B), 1)
    for start in range(0, size, B):
        here, rest = slice(start, start + B), slice(start + B, size)
        done = slice(0, start + B)
        block_work[...] = matrix[here, here]
        block_inverse[...] = jnp.where(row == column, 1.0, 0.0).astype(F32)
        for step in range(B // STEP):
            eliminate(block_work, block_inverse, step)
        own = block_inverse[...]
        if start:
            inverse[here, 0:start] = dot_split(own, inverse[here, 0:start], 1, 0)
        inverse[here, here] = own
        if start + B < size:
            upper = dot_split(own, matrix[here, rest], 1, 0)
            matrix[rest, rest] = matrix[rest, rest] - dot_split(upper, upper, 0, 0)
            inverse[rest, done] = inverse[rest, done] - dot_split(upper, inverse[here, done], 0, 0)


def first_kernel(order, blocks, coupling, inverse_out, link_out, matrix, inverse, work, work_inverse, turned):
    first = order[0]
    matrix[...] = blocks[first].astype(F32)
    factor(matrix, inverse, work, work_inverse)
    high, low = split(inverse[...])
    inverse_out[0], inverse_out[1] = high, low

    @pl.when(first == 0)
    def _():
        turned[...] = coupling[...]

    @pl.when(first != 0)
    def _():
        turned[...] = coupling[...].astype(F32).T.astype(BF16)

    kmat = turned[...]
    link_out[...] = (dot(kmat, high, 1, 1) + dot(kmat, low, 1, 1)).astype(BF16)


def second_kernel(order, blocks, link_ref, inverse_out, cross_out, matrix, inverse, work, work_inverse):
    second = order[1]
    link = link_ref[...]
    matrix[...] = blocks[second].astype(F32) - dot(link, link, 1, 1)
    factor(matrix, inverse, work, work_inverse)
    high, low = split(inverse[...])
    inverse_out[0], inverse_out[1] = high, low
    cross_high, cross_low = split(dot(high, link, 1, 0) + dot(low, link, 1, 0))
    cross_out[0], cross_out[1] = cross_high, cross_low


def factor_scratch(size):
    return [pltpu.VMEM((size, size), F32), pltpu.VMEM((size, size), F32), pltpu.VMEM((B, B), F32), pltpu.VMEM((B, B), F32)]


def panel_call(kernel, order, blocks, third, second_shape, extra, name):
    size = blocks.shape[-1]
    return pl.pallas_call(
        kernel,
        out_shape=(jax.ShapeDtypeStruct((2, size, size), BF16), jax.ShapeDtypeStruct(second_shape, BF16)),
        in_specs=[SMEM, VMEM, VMEM],
        out_specs=(VMEM, VMEM),
        scratch_shapes=factor_scratch(size) + extra,
        cost_estimate=pl.CostEstimate(flops=20_000_000_000, transcendentals=0, bytes_accessed=8_000_000),
        name=name,
    )(order, blocks, third)


def keep_of(pattern, lookup, panel, slot):
    return pattern[panel, lookup[slot]] == 1


def masked_rows(value, pattern, lookup, panel, first_slot):
    blocks = [
        jnp.where(keep_of(pattern, lookup, panel, first_slot + i), value[i * B : (i + 1) * B], jnp.zeros((), value.dtype))
        for i in range(value.shape[0] // B)
    ]
    return jnp.concatenate(blocks, 0)


def tail_kernel(
    order, place, pattern, lookup, own, mine, other, inverse_first, inverse_second, cross, trailing, updated, factor_out, row_rows
):
    first, second = order[0], order[1]
    row_index, col_index, core = place[0], place[1], place[2]
    height = trailing.shape[0]
    slots = height // B
    size = own.shape[-1]

    def solved(panel_first, panel_second, first_slot):
        rows_first = masked_rows(panel_first, pattern, lookup, first, first_slot)
        rows_second = masked_rows(panel_second, pattern, lookup, second, first_slot)
        leading = (dot(rows_first, inverse_first[0], 1, 1) + dot(rows_first, inverse_first[1], 1, 1)).astype(BF16)
        later = dot(rows_second, inverse_second[0], 1, 1) + dot(rows_second, inverse_second[1], 1, 1)
        later = later - dot(leading, cross[0], 1, 1) - dot(leading, cross[1], 1, 1)
        return leading, later.astype(BF16)

    own_first = own[:, first].reshape(height, size)
    own_second = own[:, second].reshape(height, size)
    leading, later = solved(own_first, own_second, row_index * slots)
    row_rows[0], row_rows[1] = leading, later
    width = factor_out.shape[1]
    offset = pl.multiple_of(col_index * width, 16)
    factor_out[first] = row_rows[0, pl.ds(offset, width), :]
    factor_out[second] = row_rows[1, pl.ds(offset, width), :]
    swapped = first != core
    mine_rows, other_rows = mine[...].reshape(height, size), other[...].reshape(height, size)
    panel_first = jnp.where(swapped, other_rows, mine_rows)
    panel_second = jnp.where(swapped, mine_rows, other_rows)
    column_leading, column_later = solved(panel_first, panel_second, col_index * slots)
    result = trailing[...].astype(F32) - dot(leading, column_leading, 1, 1) - dot(later, column_later, 1, 1)
    updated[...] = result.astype(BF16)


def local(
    trailing,
    offdiagonal_panel_rows,
    pivot_diagonal_blocks,
    coupling,
    pattern,
    block_slot_lookup,
    elimination_sequence,
):
    depth, cores, columns = lax.axis_size("z"), lax.axis_size("core"), lax.axis_size("col")
    row_index = lax.axis_index("z") * cores + lax.axis_index("core")
    col_index = lax.axis_index("col")
    place = jnp.stack([row_index, col_index, lax.axis_index("core")]).astype(jnp.int32)
    rows = offdiagonal_panel_rows
    size = rows.shape[-1]
    sent = []
    for panel in range(2):
        pairs = [
            (source * columns + j, (cores * j + panel) * columns + source)
            for source in range(columns)
            for j in range(columns)
        ]
        sent.append(lax.ppermute(rows[panel], ("z", "core", "col"), pairs))
    piece = jnp.where(lax.axis_index("core") == 0, sent[0], sent[1])
    own = lax.all_to_all(jnp.broadcast_to(rows[None], (columns, *rows.shape)), "col", 0, 0)
    mine = lax.all_to_all(jnp.broadcast_to(piece[None], (depth, *piece.shape)), "z", 0, 0)
    other = lax.ppermute(mine, "core", [(0, 1), (1, 0)])
    inverse_first, link = panel_call(
        first_kernel, elimination_sequence, pivot_diagonal_blocks, coupling, (size, size), [pltpu.VMEM((size, size), BF16)], "first_panel"
    )
    inverse_second, cross = panel_call(
        second_kernel, elimination_sequence, pivot_diagonal_blocks, link, (2, size, size), [], "second_panel"
    )
    return pl.pallas_call(
        tail_kernel,
        out_shape=(
            jax.ShapeDtypeStruct(trailing.shape, BF16),
            jax.ShapeDtypeStruct(rows.shape, BF16),
        ),
        in_specs=[SMEM] * 4 + [VMEM] * 7,
        out_specs=(VMEM, VMEM),
        scratch_shapes=[pltpu.VMEM((2, trailing.shape[0], size), BF16)],
        name="trailing_update",
    )(
        elimination_sequence, place, pattern, block_slot_lookup, own, mine, other,
        inverse_first, inverse_second, cross, trailing,
    )


def solution(mesh):
    chips = mesh.shape["row"] // 2
    split_mesh = Mesh(mesh.devices.reshape(chips, 2, mesh.shape["col"]), ("z", "core", "col"))
    row = ("z", "core")
    panels = P(None, ("z", "core", "col"), None)
    return jax.shard_map(
        local,
        mesh=split_mesh,
        in_specs=(P(row, "col"), panels, P(), P(), P(), P(), P()),
        out_specs=(P(row, "col"), panels),
        check_vma=False,
    )
```

```python
import jax
import jax.numpy as jnp
from jax import lax
from jax.experimental import pallas as pl
from jax.experimental.pallas import tpu as pltpu
from jax.sharding import Mesh, PartitionSpec as P


B = 128
STEP = 16
CHUNK = 384
F32 = jnp.float32
BF16 = jnp.bfloat16


VMEM = pl.BlockSpec(memory_space=pltpu.VMEM)
SMEM = pl.BlockSpec(memory_space=pltpu.SMEM)
ANY = pl.BlockSpec(memory_space=pl.ANY)


def dot(left, right, contract_left, contract_right):
    return lax.dot_general(
        left, right, (((contract_left,), (contract_right,)), ((), ())), preferred_element_type=F32
    )


def split(value):
    high = value.astype(BF16)
    return high, (value - high.astype(F32)).astype(BF16)


def dot_split(left, right, contract_left, contract_right):
    left_high, left_low = split(left)
    right_high, right_low = split(right)
    return (
        dot(left_high, right_high, contract_left, contract_right)
        + dot(left_high, right_low, contract_left, contract_right)
        + dot(left_low, right_high, contract_left, contract_right)
    )


def row_of(value, sublane):
    return jnp.broadcast_to(value[sublane : sublane + 1, :], value.shape)


def eliminate(work, inverse, step):
    start = STEP * step
    tiles = STEP // 8
    rows = [[ref[start + 8 * h : start + 8 * h + 8, :] for h in range(tiles)] for ref in (work, inverse)]
    columns = [
        [
            jnp.broadcast_to(rows[0][h][:, start + j : start + j + 1], (8, B)) if h >= j // 8 else None
            for h in range(tiles)
        ]
        for j in range(STEP)
    ]
    nothing = jnp.minimum(jnp.abs(rows[0][0]), 0.0)
    columns[0] = [column + nothing for column in columns[0]]
    sublane = lax.broadcasted_iota(jnp.int32, (8, B), 0)
    zero = jnp.zeros((8, B), F32)
    scale = [zero] * tiles
    for k in range(STEP):
        tile, s = k // 8, k % 8
        pivot = list(columns[k])
        root = lax.rsqrt(row_of(pivot[tile], s))
        inverse_pivot = root * root
        scale[tile] = jnp.where(sublane == s, root, scale[tile])
        below = [(h, pivot[h]) for h in range(tile + 1, tiles)]
        if s < 7:
            below.append((tile, jnp.where(sublane > s, pivot[tile], zero)))
        for j in range(k + 1, STEP):
            entry = row_of(pivot[j // 8], j % 8)
            if j > k + 1:
                entry = entry * inverse_pivot
            for h, column in below:
                if h >= j // 8:
                    change = column * entry
                    columns[j][h] = columns[j][h] - (change if j > k + 1 else change * inverse_pivot)
        for side in rows:
            pivot_row = row_of(side[tile], s) * inverse_pivot
            for h, column in below:
                side[h] = side[h] - column * pivot_row
    rows = [jnp.concatenate([side[h] * scale[h] for h in range(tiles)], 0) for side in rows]
    work[start : start + STEP, :] = rows[0]
    inverse[start : start + STEP, :] = rows[1]
    if start + STEP == B:
        return
    upper_high, upper_low = split(rows[0])
    side_high, side_low = split(rows[1])
    left = jnp.concatenate([upper_high, upper_high, upper_low], 0)
    rest = slice(start + STEP, B)
    change = dot(left, jnp.concatenate([upper_high, upper_low, upper_high], 0), 0, 0)
    work[rest, :] = work[rest, :] - change[rest, :]
    change = dot(left, jnp.concatenate([side_high, side_low, side_high], 0), 0, 0)
    inverse[rest, :] = inverse[rest, :] - change[rest, :]


def factor(matrix, inverse, block_work, block_inverse):
    size = matrix.shape[0]
    inverse[...] = jnp.zeros(inverse.shape, F32)
    row = lax.broadcasted_iota(jnp.int32, (B, B), 0)
    column = lax.broadcasted_iota(jnp.int32, (B, B), 1)
    for start in range(0, size, B):
        here, rest = slice(start, start + B), slice(start + B, size)
        done = slice(0, start + B)
        block_work[...] = matrix[here, here]
        block_inverse[...] = jnp.where(row == column, 1.0, 0.0).astype(F32)
        for step in range(B // STEP):
            eliminate(block_work, block_inverse, step)
        own = block_inverse[...]
        if start:
            inverse[here, 0:start] = dot_split(own, inverse[here, 0:start], 1, 0)
        inverse[here, here] = own
        if start + B < size:
            upper = dot_split(own, matrix[here, rest], 1, 0)
            matrix[rest, rest] = matrix[rest, rest] - dot_split(upper, upper, 0, 0)
            inverse[rest, done] = inverse[rest, done] - dot_split(upper, inverse[here, done], 0, 0)


def first_kernel(order, blocks, coupling, inverse_out, link_out, matrix, inverse, work, work_inverse, turned):
    first = order[0]
    matrix[...] = blocks[first].astype(F32)
    factor(matrix, inverse, work, work_inverse)
    high, low = split(inverse[...])
    inverse_out[0], inverse_out[1] = high, low

    @pl.when(first == 0)
    def _():
        turned[...] = coupling[...]

    @pl.when(first != 0)
    def _():
        turned[...] = coupling[...].astype(F32).T.astype(BF16)

    kmat = turned[...]
    link_out[...] = (dot(kmat, high, 1, 1) + dot(kmat, low, 1, 1)).astype(BF16)


def second_kernel(order, blocks, link_ref, inverse_out, matrix, inverse, work, work_inverse):
    second = order[1]
    link = link_ref[...]
    matrix[...] = blocks[second].astype(F32) - dot(link, link, 1, 1)
    factor(matrix, inverse, work, work_inverse)
    inverse_out[0], inverse_out[1] = split(inverse[...])


def factor_scratch(size):
    return [pltpu.VMEM((size, size), F32), pltpu.VMEM((size, size), F32), pltpu.VMEM((B, B), F32), pltpu.VMEM((B, B), F32)]


def panel_call(kernel, order, blocks, third, with_link, extra):
    size = blocks.shape[-1]
    shapes = [jax.ShapeDtypeStruct((2, size, size), BF16)]
    if with_link:
        shapes.append(jax.ShapeDtypeStruct((size, size), BF16))
    return pl.pallas_call(
        kernel,
        out_shape=shapes,
        in_specs=[SMEM, VMEM, VMEM],
        out_specs=[VMEM] * len(shapes),
        scratch_shapes=factor_scratch(size) + extra,
        cost_estimate=pl.CostEstimate(flops=20_000_000_000, transcendentals=0, bytes_accessed=8_000_000),
    )(order, blocks, third)


def keep_of(pattern, lookup, panel, slot):
    return pattern[panel, lookup[slot]] == 1


def masked(value, pattern, lookup, panel, slot):
    blocks = [
        jnp.where(keep_of(pattern, lookup, panel, slot + i), value[i * B : (i + 1) * B], jnp.zeros((), value.dtype))
        for i in range(value.shape[0] // B)
    ]
    return jnp.concatenate(blocks, 0)


def solved(rows_first, rows_second, inverse_first, inverse_second, link):
    leading = (dot(rows_first, inverse_first[0], 1, 1) + dot(rows_first, inverse_first[1], 1, 1)).astype(BF16)
    high, low = split(rows_second.astype(F32) - dot(leading, link[...], 1, 1))
    later = dot(high, inverse_second[0], 1, 1) + dot(high, inverse_second[1], 1, 1) + dot(low, inverse_second[0], 1, 1)
    return leading, later.astype(BF16)


def started(sources, targets, semaphores):
    copies = [pltpu.make_async_copy(s, t, semaphores.at[i]) for i, (s, t) in enumerate(zip(sources, targets))]
    for copy in copies:
        copy.start()
    return copies


def own_kernel(
    order, place, pattern, lookup, own_hbm, inverse_first_hbm, link_hbm, inverse_second_hbm, row_rows_hbm, factor_out,
    own, inverse_first, link, inverse_second, row_rows, semaphores,
):
    first, second = order[0], order[1]
    height, size = row_rows.shape[1:]
    slot = place[0] * (height // B)
    pieces = own.shape[0]
    width = height // pieces
    copies = started(
        (own_hbm, inverse_first_hbm, link_hbm, inverse_second_hbm), (own, inverse_first, link, inverse_second), semaphores
    )
    for copy in copies:
        copy.wait()
    out = []
    step = CHUNK // width
    for start in range(0, height, CHUNK):
        part = pl.ds(start // width, step)
        rows_first, rows_second = [
            masked(own[part, panel].reshape(CHUNK, size), pattern, lookup, panel, slot + start // B)
            for panel in (first, second)
        ]
        here = slice(start, start + CHUNK)
        row_rows[0, here], row_rows[1, here] = solved(rows_first, rows_second, inverse_first, inverse_second, link)
        i = len(copies) + start // CHUNK
        copy = pltpu.make_async_copy(
            row_rows.at[:, pl.ds(start, CHUNK)], row_rows_hbm.at[:, pl.ds(start, CHUNK)], semaphores.at[i]
        )
        copy.start()
        out.append(copy)
    offset = pl.multiple_of(place[1] * width, 16)
    factor_out[first] = row_rows[0, pl.ds(offset, width), :]
    factor_out[second] = row_rows[1, pl.ds(offset, width), :]
    for copy in out:
        copy.wait()


def tail_kernel(
    order, place, pattern, lookup,
    mine_hbm, other_hbm, inverse_first_hbm, link_hbm, inverse_second_hbm, row_rows_hbm, trailing_hbm, updated_hbm,
    columns, inverse_first, link, inverse_second, row_rows, trailing, column_rows, updated, semaphores,
):
    first, second = order[0], order[1]
    core = place[2]
    height = trailing.shape[0]
    size = column_rows.shape[-1]
    slot = place[1] * (height // B)
    pieces = columns.shape[1]
    width = height // pieces
    copies = started(
        (mine_hbm, other_hbm, inverse_first_hbm, link_hbm, inverse_second_hbm, row_rows_hbm, trailing_hbm),
        (columns.at[core], columns.at[1 - core], inverse_first, link, inverse_second, row_rows, trailing),
        semaphores,
    )
    for copy in copies[:5]:
        copy.wait()
    step = CHUNK // width
    for start in range(0, height, CHUNK):
        part = pl.ds(start // width, step)
        rows_first, rows_second = [
            masked(columns[panel, part].reshape(CHUNK, size), pattern, lookup, panel, slot + start // B)
            for panel in (first, second)
        ]
        here = slice(start, start + CHUNK)
        column_rows[0, here], column_rows[1, here] = solved(
            rows_first, rows_second, inverse_first, inverse_second, link
        )
    for copy in copies[5:]:
        copy.wait()
    out = []
    for start in range(0, height, CHUNK):
        here = slice(start, start + CHUNK)
        result = trailing[here].astype(F32) - dot(row_rows[0, here], column_rows[0], 1, 1)
        result = result - dot(row_rows[1, here], column_rows[1], 1, 1)
        updated[here] = result.astype(BF16)
        chunk = pl.ds(start, CHUNK)
        copy = pltpu.make_async_copy(
            updated.at[chunk], updated_hbm.at[chunk], semaphores.at[len(copies) + start // CHUNK]
        )
        copy.start()
        out.append(copy)
    for copy in out:
        copy.wait()


def local(
    trailing,
    offdiagonal_panel_rows,
    pivot_diagonal_blocks,
    coupling,
    pattern,
    block_slot_lookup,
    elimination_sequence,
):
    depth, cores, columns = lax.axis_size("z"), lax.axis_size("core"), lax.axis_size("col")
    col_index, core = lax.axis_index("col"), lax.axis_index("core")
    place = jnp.stack([lax.axis_index("z") * cores + core, col_index, core]).astype(jnp.int32)
    rows = offdiagonal_panel_rows
    size = rows.shape[-1]
    height = trailing.shape[0]
    everywhere = ("z", "core", "col")

    def device(z, k, j):
        return (z * cores + k) * columns + j

    own = lax.all_to_all(jnp.broadcast_to(rows[None], (columns, *rows.shape)), "col", 0, 0)
    sent = []
    for panel in range(2):
        pairs = [
            (device(c // cores, c % cores, j), device(j, panel, c))
            for c in range(columns)
            for j in range(columns)
        ]
        sent.append(lax.ppermute(rows[panel], everywhere, pairs))
    piece = jnp.where(core == 0, sent[0], sent[1])
    mine = lax.all_to_all(jnp.broadcast_to(piece[None], (depth, *piece.shape)), "z", 0, 0)
    inverse_first, link = panel_call(
        first_kernel, elimination_sequence, pivot_diagonal_blocks, coupling, True,
        [pltpu.VMEM((size, size), BF16)],
    )
    (inverse_second,) = panel_call(second_kernel, elimination_sequence, pivot_diagonal_blocks, link, False, [])
    other = lax.ppermute(mine, "core", [(0, 1), (1, 0)])
    scalars = (elimination_sequence, place, pattern, block_slot_lookup)
    chunks = height // CHUNK
    square = pltpu.VMEM((2, size, size), BF16)
    solving = [square, pltpu.VMEM((size, size), BF16), square, pltpu.VMEM((2, height, size), BF16)]
    tile = pltpu.VMEM(trailing.shape, BF16)
    row_rows, factor_out = pl.pallas_call(
        own_kernel,
        out_shape=(jax.ShapeDtypeStruct((2, height, size), BF16), jax.ShapeDtypeStruct(rows.shape, BF16)),
        in_specs=[SMEM] * 4 + [ANY] * 4,
        out_specs=(ANY, VMEM),
        scratch_shapes=[pltpu.VMEM(own.shape, BF16)] + solving + [pltpu.SemaphoreType.DMA((4 + chunks,))],
        name="own_rows",
    )(*scalars, own, inverse_first, link, inverse_second)
    updated = pl.pallas_call(
        tail_kernel,
        out_shape=jax.ShapeDtypeStruct(trailing.shape, BF16),
        in_specs=[SMEM] * 4 + [ANY] * 7,
        out_specs=ANY,
        scratch_shapes=[pltpu.VMEM((2, *mine.shape), BF16)]
        + solving
        + [tile, pltpu.VMEM((2, height, size), BF16), tile, pltpu.SemaphoreType.DMA((7 + chunks,))],
        name="trailing_update",
    )(*scalars, mine, other, inverse_first, link, inverse_second, row_rows, trailing)
    return updated, factor_out


def solution(mesh):
    chips = mesh.shape["row"] // 2
    split_mesh = Mesh(mesh.devices.reshape(chips, 2, mesh.shape["col"]), ("z", "core", "col"))
    row = ("z", "core")
    panels = P(None, ("z", "core", "col"), None)
    return jax.shard_map(
        local,
        mesh=split_mesh,
        in_specs=(P(row, "col"), panels, P(), P(), P(), P(), P()),
        out_specs=(P(row, "col"), panels),
        check_vma=False,
    )
```

```python
import jax
import jax.numpy as jnp
from jax import lax
from jax.experimental import pallas as pl
from jax.experimental.pallas import tpu as pltpu
from jax.sharding import Mesh, PartitionSpec as P


B = 128
STEP = 16
CHUNK = 384
F32 = jnp.float32
BF16 = jnp.bfloat16


VMEM = pl.BlockSpec(memory_space=pltpu.VMEM)
SMEM = pl.BlockSpec(memory_space=pltpu.SMEM)
ANY = pl.BlockSpec(memory_space=pl.ANY)


def dot(left, right, contract_left, contract_right):
    return lax.dot_general(
        left, right, (((contract_left,), (contract_right,)), ((), ())), preferred_element_type=F32
    )


def split(value):
    high = value.astype(BF16)
    return high, (value - high.astype(F32)).astype(BF16)


def dot_split(left, right, contract_left, contract_right):
    left_high, left_low = split(left)
    right_high, right_low = split(right)
    return (
        dot(left_high, right_high, contract_left, contract_right)
        + dot(left_high, right_low, contract_left, contract_right)
        + dot(left_low, right_high, contract_left, contract_right)
    )


def row_of(value, sublane):
    return jnp.broadcast_to(value[sublane : sublane + 1, :], value.shape)


def eliminate(work, inverse, step):
    start = STEP * step
    tiles = STEP // 8
    rows = [[ref[start + 8 * h : start + 8 * h + 8, :] for h in range(tiles)] for ref in (work, inverse)]
    columns = [
        [
            jnp.broadcast_to(rows[0][h][:, start + j : start + j + 1], (8, B)) if h >= j // 8 else None
            for h in range(tiles)
        ]
        for j in range(STEP)
    ]
    nothing = jnp.minimum(jnp.abs(rows[0][0]), 0.0)
    columns[0] = [column + nothing for column in columns[0]]
    sublane = lax.broadcasted_iota(jnp.int32, (8, B), 0)
    zero = jnp.zeros((8, B), F32)
    scale = [zero] * tiles
    for k in range(STEP):
        tile, s = k // 8, k % 8
        pivot = list(columns[k])
        root = lax.rsqrt(row_of(pivot[tile], s))
        inverse_pivot = root * root
        scale[tile] = jnp.where(sublane == s, root, scale[tile])
        below = [(h, pivot[h]) for h in range(tile + 1, tiles)]
        if s < 7:
            below.append((tile, jnp.where(sublane > s, pivot[tile], zero)))
        for j in range(k + 1, STEP):
            entry = row_of(pivot[j // 8], j % 8)
            if j > k + 1:
                entry = entry * inverse_pivot
            for h, column in below:
                if h >= j // 8:
                    change = column * entry
                    columns[j][h] = columns[j][h] - (change if j > k + 1 else change * inverse_pivot)
        for side in rows:
            pivot_row = row_of(side[tile], s) * inverse_pivot
            for h, column in below:
                side[h] = side[h] - column * pivot_row
    rows = [jnp.concatenate([side[h] * scale[h] for h in range(tiles)], 0) for side in rows]
    work[start : start + STEP, :] = rows[0]
    inverse[start : start + STEP, :] = rows[1]
    if start + STEP == B:
        return
    upper_high, upper_low = split(rows[0])
    side_high, side_low = split(rows[1])
    left = jnp.concatenate([upper_high, upper_high, upper_low], 0)
    rest = slice(start + STEP, B)
    change = dot(left, jnp.concatenate([upper_high, upper_low, upper_high], 0), 0, 0)
    work[rest, :] = work[rest, :] - change[rest, :]
    change = dot(left, jnp.concatenate([side_high, side_low, side_high], 0), 0, 0)
    inverse[rest, :] = inverse[rest, :] - change[rest, :]


def factor(matrix, inverse, block_work, block_inverse):
    size = matrix.shape[0]
    inverse[...] = jnp.zeros(inverse.shape, F32)
    row = lax.broadcasted_iota(jnp.int32, (B, B), 0)
    column = lax.broadcasted_iota(jnp.int32, (B, B), 1)
    for start in range(0, size, B):
        here, rest = slice(start, start + B), slice(start + B, size)
        done = slice(0, start + B)
        block_work[...] = matrix[here, here]
        block_inverse[...] = jnp.where(row == column, 1.0, 0.0).astype(F32)
        for step in range(B // STEP):
            eliminate(block_work, block_inverse, step)
        own = block_inverse[...]
        if start:
            inverse[here, 0:start] = dot_split(own, inverse[here, 0:start], 1, 0)
        inverse[here, here] = own
        if start + B < size:
            upper = dot_split(own, matrix[here, rest], 1, 0)
            matrix[rest, rest] = matrix[rest, rest] - dot_split(upper, upper, 0, 0)
            inverse[rest, done] = inverse[rest, done] - dot_split(upper, inverse[here, done], 0, 0)


def first_half_kernel(order, blocks, top_out, left_out, rest_out, matrix, inverse, work, work_inverse):
    first = order[0]
    half = matrix.shape[0]
    top, rest = slice(0, half), slice(half, 2 * half)
    matrix[...] = blocks[first, top, top].astype(F32)
    factor(matrix, inverse, work, work_inverse)
    upper = dot_split(inverse[...], blocks[first, top, rest].astype(F32), 1, 0)
    top_out[...] = inverse[...]
    left_out[...] = -dot_split(upper, inverse[...], 0, 0)
    rest_out[...] = blocks[first, rest, rest].astype(F32) - dot_split(upper, upper, 0, 0)


def first_kernel(order, coupling, top_ref, left_ref, rest_ref, inverse_out, link_out, matrix, inverse, work, work_inverse):
    half = matrix.shape[0]
    top, rest = slice(0, half), slice(half, 2 * half)
    matrix[...] = rest_ref[...]
    factor(matrix, inverse, work, work_inverse)
    inverse_out[0, top, rest] = inverse_out[1, top, rest] = jnp.zeros((half, half), BF16)
    inverse_out[0, top, top], inverse_out[1, top, top] = split(top_ref[...])
    inverse_out[0, rest, rest], inverse_out[1, rest, rest] = split(inverse[...])
    inverse_out[0, rest, top], inverse_out[1, rest, top] = split(dot_split(inverse[...], left_ref[...], 1, 0))

    @pl.when(order[0] == 0)
    def _():
        kmat = coupling[...]
        link_out[...] = (dot(kmat, inverse_out[0], 1, 1) + dot(kmat, inverse_out[1], 1, 1)).astype(BF16)

    @pl.when(order[0] != 0)
    def _():
        kmat = coupling[...].astype(F32).T.astype(BF16)
        link_out[...] = (dot(kmat, inverse_out[0], 1, 1) + dot(kmat, inverse_out[1], 1, 1)).astype(BF16)


def second_kernel(order, blocks, link_ref, inverse_out, matrix, inverse, work, work_inverse):
    second = order[1]
    link = link_ref[...]
    matrix[...] = blocks[second].astype(F32) - dot(link, link, 1, 1)
    factor(matrix, inverse, work, work_inverse)
    inverse_out[0], inverse_out[1] = split(inverse[...])


def panel_call(kernel, operands, shapes, size):
    return pl.pallas_call(
        kernel,
        out_shape=shapes,
        in_specs=[SMEM] + [VMEM] * (len(operands) - 1),
        out_specs=[VMEM] * len(shapes),
        scratch_shapes=[pltpu.VMEM((size, size), F32)] * 2 + [pltpu.VMEM((B, B), F32)] * 2,
        cost_estimate=pl.CostEstimate(flops=10_000_000_000, transcendentals=0, bytes_accessed=4_000_000),
    )(*operands)


def keep_of(pattern, lookup, panel, slot):
    return pattern[panel, lookup[slot]] == 1


def masked(value, pattern, lookup, panel, slot):
    blocks = [
        jnp.where(keep_of(pattern, lookup, panel, slot + i), value[i * B : (i + 1) * B], jnp.zeros((), value.dtype))
        for i in range(value.shape[0] // B)
    ]
    return jnp.concatenate(blocks, 0)


def solved(rows_first, rows_second, inverse_first, inverse_second, link):
    leading = (dot(rows_first, inverse_first[0], 1, 1) + dot(rows_first, inverse_first[1], 1, 1)).astype(BF16)
    high, low = split(rows_second.astype(F32) - dot(leading, link[...], 1, 1))
    later = dot(high, inverse_second[0], 1, 1) + dot(high, inverse_second[1], 1, 1) + dot(low, inverse_second[0], 1, 1)
    return leading, later.astype(BF16)


def started(sources, targets, semaphores):
    copies = [pltpu.make_async_copy(s, t, semaphores.at[i]) for i, (s, t) in enumerate(zip(sources, targets))]
    for copy in copies:
        copy.start()
    return copies


def own_kernel(
    order, place, pattern, lookup, own_hbm, inverse_first_hbm, link_hbm, inverse_second_hbm, row_rows_hbm, factor_out,
    own, inverse_first, link, inverse_second, row_rows, semaphores,
):
    first, second = order[0], order[1]
    height, size = row_rows.shape[1:]
    slot = place[0] * (height // B)
    pieces = own.shape[0]
    width = height // pieces
    copies = started(
        (own_hbm, inverse_first_hbm, link_hbm, inverse_second_hbm), (own, inverse_first, link, inverse_second), semaphores
    )
    for copy in copies:
        copy.wait()
    out = []
    step = CHUNK // width
    for start in range(0, height, CHUNK):
        part = pl.ds(start // width, step)
        rows_first, rows_second = [
            masked(own[part, panel].reshape(CHUNK, size), pattern, lookup, panel, slot + start // B)
            for panel in (first, second)
        ]
        here = slice(start, start + CHUNK)
        row_rows[0, here], row_rows[1, here] = solved(rows_first, rows_second, inverse_first, inverse_second, link)
        i = len(copies) + start // CHUNK
        copy = pltpu.make_async_copy(
            row_rows.at[:, pl.ds(start, CHUNK)], row_rows_hbm.at[:, pl.ds(start, CHUNK)], semaphores.at[i]
        )
        copy.start()
        out.append(copy)
    offset = pl.multiple_of(place[1] * width, 16)
    factor_out[first] = row_rows[0, pl.ds(offset, width), :]
    factor_out[second] = row_rows[1, pl.ds(offset, width), :]
    for copy in out:
        copy.wait()


def tail_kernel(
    order, place, pattern, lookup,
    mine_hbm, other_hbm, inverse_first_hbm, link_hbm, inverse_second_hbm, row_rows_hbm, trailing_hbm, updated_hbm,
    columns, inverse_first, link, inverse_second, row_rows, trailing, column_rows, updated, semaphores,
):
    first, second = order[0], order[1]
    core = place[2]
    height = trailing.shape[0]
    size = column_rows.shape[-1]
    slot = place[1] * (height // B)
    pieces = columns.shape[1]
    width = height // pieces
    copies = started(
        (mine_hbm, other_hbm, inverse_first_hbm, link_hbm, inverse_second_hbm, row_rows_hbm, trailing_hbm),
        (columns.at[core], columns.at[1 - core], inverse_first, link, inverse_second, row_rows, trailing),
        semaphores,
    )
    for copy in copies[:5]:
        copy.wait()
    step = CHUNK // width
    for start in range(0, height, CHUNK):
        part = pl.ds(start // width, step)
        rows_first, rows_second = [
            masked(columns[panel, part].reshape(CHUNK, size), pattern, lookup, panel, slot + start // B)
            for panel in (first, second)
        ]
        here = slice(start, start + CHUNK)
        column_rows[0, here], column_rows[1, here] = solved(
            rows_first, rows_second, inverse_first, inverse_second, link
        )
    for copy in copies[5:]:
        copy.wait()
    out = []
    for start in range(0, height, CHUNK):
        here = slice(start, start + CHUNK)
        result = trailing[here].astype(F32) - dot(row_rows[0, here], column_rows[0], 1, 1)
        result = result - dot(row_rows[1, here], column_rows[1], 1, 1)
        updated[here] = result.astype(BF16)
        chunk = pl.ds(start, CHUNK)
        copy = pltpu.make_async_copy(
            updated.at[chunk], updated_hbm.at[chunk], semaphores.at[len(copies) + start // CHUNK]
        )
        copy.start()
        out.append(copy)
    for copy in out:
        copy.wait()


def local(
    trailing,
    offdiagonal_panel_rows,
    pivot_diagonal_blocks,
    coupling,
    pattern,
    block_slot_lookup,
    elimination_sequence,
):
    depth, cores, columns = lax.axis_size("z"), lax.axis_size("core"), lax.axis_size("col")
    col_index, core = lax.axis_index("col"), lax.axis_index("core")
    place = jnp.stack([lax.axis_index("z") * cores + core, col_index, core]).astype(jnp.int32)
    rows = offdiagonal_panel_rows
    size = rows.shape[-1]
    height = trailing.shape[0]
    everywhere = ("z", "core", "col")

    def device(z, k, j):
        return (z * cores + k) * columns + j

    own = lax.all_to_all(jnp.broadcast_to(rows[None], (columns, *rows.shape)), "col", 0, 0)
    sent = []
    for panel in range(2):
        pairs = [
            (device(c // cores, c % cores, j), device(j, panel, c))
            for c in range(columns)
            for j in range(columns)
        ]
        sent.append(lax.ppermute(rows[panel], everywhere, pairs))
    piece = jnp.where(core == 0, sent[0], sent[1])
    mine = lax.all_to_all(jnp.broadcast_to(piece[None], (depth, *piece.shape)), "z", 0, 0)
    half = jax.ShapeDtypeStruct((size // 2, size // 2), F32)
    inverse_shape = jax.ShapeDtypeStruct((2, size, size), BF16)
    halves = panel_call(first_half_kernel, (elimination_sequence, pivot_diagonal_blocks), [half] * 3, size // 2)
    inverse_first, link = panel_call(
        first_kernel, (elimination_sequence, coupling, *halves),
        [inverse_shape, jax.ShapeDtypeStruct((size, size), BF16)], size // 2,
    )
    (inverse_second,) = panel_call(
        second_kernel, (elimination_sequence, pivot_diagonal_blocks, link), [inverse_shape], size
    )
    other = lax.ppermute(mine, "core", [(0, 1), (1, 0)])
    scalars = (elimination_sequence, place, pattern, block_slot_lookup)
    chunks = height // CHUNK
    square = pltpu.VMEM((2, size, size), BF16)
    solving = [square, pltpu.VMEM((size, size), BF16), square, pltpu.VMEM((2, height, size), BF16)]
    tile = pltpu.VMEM(trailing.shape, BF16)
    row_rows, factor_out = pl.pallas_call(
        own_kernel,
        out_shape=(jax.ShapeDtypeStruct((2, height, size), BF16), jax.ShapeDtypeStruct(rows.shape, BF16)),
        in_specs=[SMEM] * 4 + [ANY] * 4,
        out_specs=(ANY, VMEM),
        scratch_shapes=[pltpu.VMEM(own.shape, BF16)] + solving + [pltpu.SemaphoreType.DMA((4 + chunks,))],
        name="own_rows",
    )(*scalars, own, inverse_first, link, inverse_second)
    updated = pl.pallas_call(
        tail_kernel,
        out_shape=jax.ShapeDtypeStruct(trailing.shape, BF16),
        in_specs=[SMEM] * 4 + [ANY] * 7,
        out_specs=ANY,
        scratch_shapes=[pltpu.VMEM((2, *mine.shape), BF16)]
        + solving
        + [tile, pltpu.VMEM((2, height, size), BF16), tile, pltpu.SemaphoreType.DMA((7 + chunks,))],
        name="trailing_update",
    )(*scalars, mine, other, inverse_first, link, inverse_second, row_rows, trailing)
    return updated, factor_out


def solution(mesh):
    chips = mesh.shape["row"] // 2
    split_mesh = Mesh(mesh.devices.reshape(chips, 2, mesh.shape["col"]), ("z", "core", "col"))
    row = ("z", "core")
    panels = P(None, ("z", "core", "col"), None)
    return jax.shard_map(
        local,
        mesh=split_mesh,
        in_specs=(P(row, "col"), panels, P(), P(), P(), P(), P()),
        out_specs=(P(row, "col"), panels),
        check_vma=False,
    )
```

```python
import math

import jax
import jax.numpy as jnp
import numpy as np
from jax import lax
from jax.experimental import pallas as pl
from jax.experimental.pallas import tpu as pltpu
from jax.sharding import Mesh, PartitionSpec as P


B = 128
STEP = 16
CHUNK = 384
F32 = jnp.float32
BF16 = jnp.bfloat16


VMEM = pl.BlockSpec(memory_space=pltpu.VMEM)
SMEM = pl.BlockSpec(memory_space=pltpu.SMEM)
ANY = pl.BlockSpec(memory_space=pl.ANY)
LIMITS = pltpu.CompilerParams(vmem_limit_bytes=32 << 20)


def dot(left, right, contract_left, contract_right):
    return lax.dot_general(
        left, right, (((contract_left,), (contract_right,)), ((), ())), preferred_element_type=F32
    )


def split(value):
    high = value.astype(BF16)
    return high, (value - high.astype(F32)).astype(BF16)


def dot_split(left, right, contract_left, contract_right):
    left_high, left_low = split(left)
    right_high, right_low = split(right)
    return (
        dot(left_high, right_high, contract_left, contract_right)
        + dot(left_high, right_low, contract_left, contract_right)
        + dot(left_low, right_high, contract_left, contract_right)
    )


def row_of(value, sublane):
    return jnp.broadcast_to(value[sublane : sublane + 1, :], value.shape)


def eliminate(work, inverse, step):
    start = STEP * step
    tiles = STEP // 8
    rows = [[ref[start + 8 * h : start + 8 * h + 8, :] for h in range(tiles)] for ref in (work, inverse)]
    columns = [
        [
            jnp.broadcast_to(rows[0][h][:, start + j : start + j + 1], (8, B)) if h >= j // 8 else None
            for h in range(tiles)
        ]
        for j in range(STEP)
    ]
    nothing = jnp.minimum(jnp.abs(rows[0][0]), 0.0)
    columns[0] = [column + nothing for column in columns[0]]
    sublane = lax.broadcasted_iota(jnp.int32, (8, B), 0)
    zero = jnp.zeros((8, B), F32)
    scale = [zero] * tiles
    for k in range(STEP):
        tile, s = k // 8, k % 8
        pivot = list(columns[k])
        root = lax.rsqrt(row_of(pivot[tile], s))
        inverse_pivot = root * root
        scale[tile] = jnp.where(sublane == s, root, scale[tile])
        below = [(h, pivot[h]) for h in range(tile + 1, tiles)]
        if s < 7:
            below.append((tile, jnp.where(sublane > s, pivot[tile], zero)))
        for j in range(k + 1, STEP):
            entry = row_of(pivot[j // 8], j % 8)
            if j > k + 1:
                entry = entry * inverse_pivot
            for h, column in below:
                if h >= j // 8:
                    change = column * entry
                    columns[j][h] = columns[j][h] - (change if j > k + 1 else change * inverse_pivot)
        for side in rows:
            pivot_row = row_of(side[tile], s) * inverse_pivot
            for h, column in below:
                side[h] = side[h] - column * pivot_row
    rows = [jnp.concatenate([side[h] * scale[h] for h in range(tiles)], 0) for side in rows]
    work[start : start + STEP, :] = rows[0]
    inverse[start : start + STEP, :] = rows[1]
    if start + STEP == B:
        return
    upper_high, upper_low = split(rows[0])
    side_high, side_low = split(rows[1])
    left = jnp.concatenate([upper_high, upper_high, upper_low], 0)
    rest = slice(start + STEP, B)
    change = dot(left, jnp.concatenate([upper_high, upper_low, upper_high], 0), 0, 0)
    work[rest, :] = work[rest, :] - change[rest, :]
    change = dot(left, jnp.concatenate([side_high, side_low, side_high], 0), 0, 0)
    inverse[rest, :] = inverse[rest, :] - change[rest, :]


def factor(matrix, inverse, block_work, block_inverse):
    size = matrix.shape[0]
    inverse[...] = jnp.zeros(inverse.shape, F32)
    row = lax.broadcasted_iota(jnp.int32, (B, B), 0)
    column = lax.broadcasted_iota(jnp.int32, (B, B), 1)
    for start in range(0, size, B):
        here, rest = slice(start, start + B), slice(start + B, size)
        done = slice(0, start + B)
        block_work[...] = matrix[here, here]
        block_inverse[...] = jnp.where(row == column, 1.0, 0.0).astype(F32)
        for step in range(B // STEP):
            eliminate(block_work, block_inverse, step)
        own = block_inverse[...]
        if start:
            inverse[here, 0:start] = dot_split(own, inverse[here, 0:start], 1, 0)
        inverse[here, here] = own
        if start + B < size:
            upper = dot_split(own, matrix[here, rest], 1, 0)
            matrix[rest, rest] = matrix[rest, rest] - dot_split(upper, upper, 0, 0)
            inverse[rest, done] = inverse[rest, done] - dot_split(upper, inverse[here, done], 0, 0)


def first_half_kernel(order, blocks, top_out, left_out, rest_out, matrix, inverse, work, work_inverse):
    first = order[0]
    half = matrix.shape[0]
    top, rest = slice(0, half), slice(half, 2 * half)
    matrix[...] = blocks[first, top, top].astype(F32)
    factor(matrix, inverse, work, work_inverse)
    upper = dot_split(inverse[...], blocks[first, top, rest].astype(F32), 1, 0)
    top_out[...] = inverse[...]
    left_out[...] = -dot_split(upper, inverse[...], 0, 0)
    rest_out[...] = blocks[first, rest, rest].astype(F32) - dot_split(upper, upper, 0, 0)


def first_kernel(order, coupling, top_ref, left_ref, rest_ref, inverse_out, link_out, matrix, inverse, work, work_inverse):
    half = matrix.shape[0]
    top, rest = slice(0, half), slice(half, 2 * half)
    matrix[...] = rest_ref[...]
    factor(matrix, inverse, work, work_inverse)
    inverse_out[0, top, rest] = inverse_out[1, top, rest] = jnp.zeros((half, half), BF16)
    inverse_out[0, top, top], inverse_out[1, top, top] = split(top_ref[...])
    inverse_out[0, rest, rest], inverse_out[1, rest, rest] = split(inverse[...])
    inverse_out[0, rest, top], inverse_out[1, rest, top] = split(dot_split(inverse[...], left_ref[...], 1, 0))

    @pl.when(order[0] == 0)
    def _():
        kmat = coupling[...]
        link_out[...] = (dot(kmat, inverse_out[0], 1, 1) + dot(kmat, inverse_out[1], 1, 1)).astype(BF16)

    @pl.when(order[0] != 0)
    def _():
        kmat = coupling[...].astype(F32).T.astype(BF16)
        link_out[...] = (dot(kmat, inverse_out[0], 1, 1) + dot(kmat, inverse_out[1], 1, 1)).astype(BF16)


def second_kernel(order, blocks, link_ref, inverse_out, matrix, inverse, work, work_inverse):
    second = order[1]
    link = link_ref[...]
    matrix[...] = blocks[second].astype(F32) - dot(link, link, 1, 1)
    factor(matrix, inverse, work, work_inverse)
    inverse_out[0], inverse_out[1] = split(inverse[...])


def panel_call(kernel, operands, shapes, size):
    return pl.pallas_call(
        kernel,
        out_shape=shapes,
        in_specs=[SMEM] + [VMEM] * (len(operands) - 1),
        out_specs=[VMEM] * len(shapes),
        scratch_shapes=[pltpu.VMEM((size, size), F32)] * 2 + [pltpu.VMEM((B, B), F32)] * 2,
        cost_estimate=pl.CostEstimate(flops=10_000_000_000, transcendentals=0, bytes_accessed=4_000_000),
        compiler_params=LIMITS,
    )(*operands)


def near(value):
    return pltpu.with_memory_space_constraint(value, pltpu.VMEM)


def far(value):
    return pltpu.with_memory_space_constraint(value, pltpu.HBM)


def keep_of(pattern, lookup, panel, slot):
    return pattern[panel, lookup[slot]] == 1


def masked(value, pattern, lookup, panel, slot):
    blocks = [
        jnp.where(keep_of(pattern, lookup, panel, slot + i), value[i * B : (i + 1) * B], jnp.zeros((), value.dtype))
        for i in range(value.shape[0] // B)
    ]
    return jnp.concatenate(blocks, 0)


def solved(rows_first, rows_second, inverse_first, inverse_second, link):
    leading = (dot(rows_first, inverse_first[0], 1, 1) + dot(rows_first, inverse_first[1], 1, 1)).astype(BF16)
    high, low = split(rows_second.astype(F32) - dot(leading, link[...], 1, 1))
    later = dot(high, inverse_second[0], 1, 1) + dot(high, inverse_second[1], 1, 1) + dot(low, inverse_second[0], 1, 1)
    return leading, later.astype(BF16)


def own_kernel(
    order, place, pattern, lookup, own, inverse_first, link, inverse_second, row_rows, factor_out
):
    first, second = order[0], order[1]
    height, size = row_rows.shape[1:]
    slot = place[0] * (height // B)
    pieces = own.shape[0]
    width = height // pieces
    rows_first, rows_second = [
        masked(own[:, panel].reshape(height, size), pattern, lookup, panel, slot) for panel in (first, second)
    ]
    row_rows[0], row_rows[1] = solved(rows_first, rows_second, inverse_first, inverse_second, link)
    offset = pl.multiple_of(place[1] * width, 16)
    factor_out[first] = row_rows[0, pl.ds(offset, width), :]
    factor_out[second] = row_rows[1, pl.ds(offset, width), :]


def tail_kernel(
    order, place, pattern, lookup, plane_of,
    mine, other, inverse_first_hbm, link_hbm, inverse_second_hbm, row_rows_hbm, trailing_hbm, updated_hbm,
    inverse_first, link, inverse_second, row_rows, trailing, updated, semaphores,
):
    first, second = order[0], order[1]
    core = place[2]
    height = trailing.shape[0]
    slot = place[1] * (height // B)
    sources = (inverse_first_hbm, link_hbm, inverse_second_hbm, row_rows_hbm, trailing_hbm)
    targets = (inverse_first, link, inverse_second, row_rows, trailing)
    copies = [pltpu.make_async_copy(s, t, semaphores.at[i]) for i, (s, t) in enumerate(zip(sources, targets))]
    for copy in copies:
        copy.start()
    pieces = mine.shape[0]
    mine_rows, other_rows = [
        jnp.concatenate([ref[plane_of[place[1], j]] for j in range(pieces)], 0) for ref in (mine, other)
    ]
    rows_first = masked(jnp.where(first == core, mine_rows, other_rows), pattern, lookup, first, slot)
    rows_second = masked(jnp.where(first == core, other_rows, mine_rows), pattern, lookup, second, slot)
    for copy in copies[:3]:
        copy.wait()
    leading, later = solved(rows_first, rows_second, inverse_first, inverse_second, link)
    for copy in copies[3:]:
        copy.wait()
    out = []
    for start in range(0, height, CHUNK):
        here = slice(start, start + CHUNK)
        result = trailing[here].astype(F32) - dot(row_rows[0, here], leading, 1, 1)
        updated[here] = (result - dot(row_rows[1, here], later, 1, 1)).astype(BF16)
        chunk = pl.ds(start, CHUNK)
        copy = pltpu.make_async_copy(
            updated.at[chunk], updated_hbm.at[chunk], semaphores.at[len(copies) + start // CHUNK]
        )
        copy.start()
        out.append(copy)
    for copy in out:
        copy.wait()


def planes(columns, depth, cores):
    side = math.isqrt(columns)

    def ring(a, b, length):
        return min((a - b) % length, (b - a) % length)

    table = np.zeros((columns, columns), np.int32)
    for c in range(columns):
        across = sorted(range(columns), key=lambda j: (ring(j // side, c // side, side) + ring(j % side, c % side, side), j))
        along = sorted(range(depth), key=lambda z: (-ring(z, c // cores, depth), z))
        for j, z in zip(across, along):
            table[c, j] = z
    return table


def local(
    trailing,
    offdiagonal_panel_rows,
    pivot_diagonal_blocks,
    coupling,
    pattern,
    block_slot_lookup,
    elimination_sequence,
):
    depth, cores, columns = lax.axis_size("z"), lax.axis_size("core"), lax.axis_size("col")
    col_index, core = lax.axis_index("col"), lax.axis_index("core")
    place = jnp.stack([lax.axis_index("z") * cores + core, col_index, core]).astype(jnp.int32)
    rows = offdiagonal_panel_rows
    size = rows.shape[-1]
    height = trailing.shape[0]
    everywhere = ("z", "core", "col")

    def device(z, k, j):
        return (z * cores + k) * columns + j

    plane_of = planes(columns, depth, cores)
    place_of = jnp.asarray(plane_of, jnp.int32)
    own = lax.all_to_all(jnp.broadcast_to(rows[None], (columns, *rows.shape)), "col", 0, 0)
    sent = []
    for panel in range(2):
        pairs = [
            (device(c // cores, c % cores, j), device(int(plane_of[c, j]), panel, c))
            for c in range(columns)
            for j in range(columns)
        ]
        sent.append(lax.ppermute(rows[panel], everywhere, pairs))
    piece = sent[0] + sent[1]
    mine = lax.all_to_all(jnp.broadcast_to(piece[None], (depth, *piece.shape)), "z", 0, 0)
    half = jax.ShapeDtypeStruct((size // 2, size // 2), F32)
    inverse_shape = jax.ShapeDtypeStruct((2, size, size), BF16)
    halves = panel_call(first_half_kernel, (elimination_sequence, pivot_diagonal_blocks), [half] * 3, size // 2)
    inverse_first, link = panel_call(
        first_kernel, (elimination_sequence, *[far(value) for value in (coupling, *halves)]),
        [inverse_shape, jax.ShapeDtypeStruct((size, size), BF16)], size // 2,
    )
    (inverse_second,) = panel_call(
        second_kernel, (elimination_sequence, pivot_diagonal_blocks, link), [inverse_shape], size
    )
    other = lax.ppermute(mine, "core", [(0, 1), (1, 0)])
    scalars = (elimination_sequence, place, pattern, block_slot_lookup)
    chunks = height // CHUNK
    tile = pltpu.VMEM(trailing.shape, BF16)
    solving = (inverse_first, link, inverse_second)
    row_rows, factor_out = pl.pallas_call(
        own_kernel,
        out_shape=(jax.ShapeDtypeStruct((2, height, size), BF16), jax.ShapeDtypeStruct(rows.shape, BF16)),
        in_specs=[SMEM] * 4 + [VMEM] * 4,
        out_specs=(VMEM, VMEM),
        compiler_params=LIMITS,
        name="own_rows",
    )(*scalars, near(own), *solving)
    square = pltpu.VMEM((2, size, size), BF16)
    updated = pl.pallas_call(
        tail_kernel,
        out_shape=jax.ShapeDtypeStruct(trailing.shape, BF16),
        in_specs=[SMEM] * 5 + [VMEM] * 2 + [ANY] * 5,
        out_specs=ANY,
        scratch_shapes=[
            square, pltpu.VMEM((size, size), BF16), square, pltpu.VMEM((2, height, size), BF16), tile, tile,
            pltpu.SemaphoreType.DMA((5 + chunks,)),
        ],
        compiler_params=LIMITS,
        name="trailing_update",
    )(*scalars, place_of, near(mine), near(other), *[far(v) for v in (*solving, row_rows, trailing)])
    return updated, factor_out


def solution(mesh):
    chips = mesh.shape["row"] // 2
    split_mesh = Mesh(mesh.devices.reshape(chips, 2, mesh.shape["col"]), ("z", "core", "col"))
    row = ("z", "core")
    panels = P(None, ("z", "core", "col"), None)
    return jax.shard_map(
        local,
        mesh=split_mesh,
        in_specs=(P(row, "col"), panels, P(), P(), P(), P(), P()),
        out_specs=(P(row, "col"), panels),
        check_vma=False,
    )
```
